32 devices in a mesh: pole: 2 (over x), row: 8 (over z, y), col: 2 (over core).
Axes of the slice: x: 2, y: 2, z: 4, core: 2. Of those that a mesh axis runs over, the one named last changes fastest.
Arguments:
- panel: bfloat16 [4, 8, 2, 512, 128], P(('pole', 'col'), None, None, 'row'), parts along dimension 0, may hold values from -6 to 6
- tiles: bfloat16 [352, 2, 512, 512], P(('pole', 'row', 'col')), parts along dimension 0, may hold values from -0.078125 to 0.078125
- tile_slot: int32 [352], P(('pole', 'row', 'col')), parts along dimension 0, may hold values from 0 to 1
- tile_col: int32 [352], P(('pole', 'row', 'col')), parts along dimension 0, may hold values from 0 to 7
- pole_weight: float32 [4], P('pole'), parts along dimension 0, may hold values from -4 to 4
- box_orbitals: int32 [64, 256], P(('pole', 'row', 'col')), parts along dimension 0, may hold values from 0 to 8191, as said below
- box_basis: bfloat16 [64, 256, 512], P(('pole', 'row', 'col')), parts along dimension 0, may hold values from -0.375 to 0.375
- supernode_basis: bfloat16 [64, 128, 512], P(('pole', 'row', 'col')), parts along dimension 0, may hold values from -0.5 to 0.5
Outputs:
- inverse_column: float32 [32, 2, 512, 128], P(('pole', 'row'), None, 'col'), parts along dimension 0
- density: float32 [64, 512], P(('pole', 'row', 'col')), parts along dimension 0
The draws below stay inside these ranges and needn't reach their ends.
There are 2 independent parts, one for each index of `pole`. The reference program is written for one: setup_inputs(seed, part) draws one part's arguments, and reference() takes and returns one part's arrays. A program takes and returns all parts, laid end to end along the dimension named above; each array names one. Nothing has to cross between parts.
Inputs may be any that keep to these rules, and one draw needn't show every extreme that they name: `box_orbitals`: let a row g be held by device r * 2 + c where r = (g // 512) // 2 and c = (g % 512) // (512 // 2). The 2 boxes of one device take at most 64 rows (counted with repeats) held by any one device, and exactly 64 from some device.
All inputs are finite; a program needn't handle non-finite values.
Results may differ from the reference program's by a relative error of at most 0.0029.
Values may be sent and summed in bfloat16 or wider, within the bound.
A program may use at most 64 MiB of HBM per device.

```python
import jax
import jax.numpy as jnp
from jax import lax

B = 512
S = 128
PTS = 512
ORB_BOX = 256
NJP = 8
BR_DEV = 2
TILE_DEV = 11
BOX_DEV = 2
TILES = 176
NBOX = 32
N_ROW = 8
N_COL = 2


def draw_box_orbitals(key, part):
    devices = N_ROW * N_COL
    per_device = BOX_DEV * ORB_BOX
    capacity = 2 * per_device // devices
    half_rows = B // N_COL
    local_total = BR_DEV * half_rows

    def one_device(device_index):
        device_key = jax.random.fold_in(key, device_index + 7919)
        subkeys = jax.random.split(device_key, 4)
        forced = jax.random.randint(subkeys[0], (), 0, devices).astype(jnp.int32)
        others = jnp.arange((devices - 1) * capacity, dtype=jnp.int32) // capacity
        others = others + (others >= forced).astype(jnp.int32)
        others = jax.random.permutation(subkeys[1], others)[:per_device - capacity]
        sources = jnp.concatenate([jnp.full((capacity,), 1, jnp.int32) * forced, others])
        sources = jax.random.permutation(subkeys[2], sources)
        local_pick = jax.random.randint(subkeys[3], (per_device,), 0, local_total).astype(jnp.int32)
        block_row = sources // N_COL * BR_DEV + local_pick // half_rows
        return block_row * B + sources % N_COL * half_rows + local_pick % half_rows
    result = jax.vmap(one_device)(jnp.arange(devices, dtype=jnp.int32))
    return result.reshape(devices * BOX_DEV, ORB_BOX).astype(jnp.int32)


def touch_ends(array, key, smallest, largest):
    longest = array.shape.index(max(array.shape))
    spots = []
    for shift in (0, 1):
        where = [jax.random.randint(jax.random.fold_in(key, axis), (), 0, length) for axis, length in enumerate(array.shape)]
        where[longest] = (where[longest] + shift) % array.shape[longest]
        spots.append(tuple(where))
    return array.at[spots[0]].set(smallest).at[spots[1]].set(largest)


def level_of(own_key, shape, cuts, low, largest):
    loudness = 1.0
    for axis_at, blocks in cuts:
        steps = jax.random.uniform(jax.random.fold_in(jax.random.fold_in(own_key, 6), axis_at), (blocks,), jnp.float32, low / len(cuts), largest / len(cuts))
        loudness = loudness * jnp.repeat(jnp.exp(steps), shape[axis_at] // blocks).reshape((-1,) + (1,) * (len(shape) - 1 - axis_at))
    return loudness


def normal_values(stream_key, shape, spread, bound, shards=(), kind=jnp.bfloat16):
    array = spread * jax.random.normal(stream_key, shape, jnp.float32)
    if shards:
        array = array * level_of(stream_key, shape, shards, -0.22, 0.18)
    return jnp.clip(array, -bound, bound).astype(kind)


def setup_inputs(seed: int = 0, part: int = 0) -> dict:
    seeds = jax.random.split(jax.random.key(seed), 9)
    part_splits = jax.random.split(jax.random.fold_in(seeds[8], part), 9)
    panel = normal_values(part_splits[0], (N_COL, NJP, 2, B, S), 1.0, 6.0, ((0, 2), (3, 8)))
    tiles = normal_values(part_splits[1], (TILES, 2, B, B), (2 * B * TILE_DEV // BR_DEV) ** -0.5, 0.078125, ((0, 16),))
    tile_slot = touch_ends(jax.random.randint(part_splits[2], (TILES,), 0, BR_DEV), jax.random.fold_in(part_splits[2], 1), 0, BR_DEV - 1).astype(jnp.int32)
    tile_col = touch_ends(jax.random.randint(part_splits[3], (TILES,), 0, NJP), jax.random.fold_in(part_splits[3], 1), 0, NJP - 1).astype(jnp.int32)
    pole_weight = normal_values(part_splits[4], (2,), 1.0, 4.0, (), jnp.float32)
    box_orbitals = draw_box_orbitals(jax.random.fold_in(jax.random.fold_in(seeds[8], part), 71), part)
    box_basis = normal_values(part_splits[6], (NBOX, ORB_BOX, PTS), ORB_BOX ** -0.5, 0.375, ((0, 16),))
    supernode_basis = normal_values(part_splits[7], (NBOX, S, PTS), S ** -0.5, 0.5, ((0, 16),))
    return {"panel": panel, "tiles": tiles, "tile_slot": tile_slot, "tile_col": tile_col, "pole_weight": pole_weight, "box_orbitals": box_orbitals, "box_basis": box_basis, "supernode_basis": supernode_basis}


def reference(panel, tiles, tile_slot, tile_col, pole_weight, box_orbitals, box_basis, supernode_basis):
    tile_total = tiles.shape[0]

    def add_tile(column, inputs):
        tile_block, slot_row, block_col, tile_index = inputs
        device = tile_index // TILE_DEV
        block_row = ((device // N_COL) * BR_DEV + slot_row).astype(jnp.int32)
        factor = panel[device % N_COL, block_col].astype(jnp.float32)
        tile_wide = tile_block.astype(jnp.float32)
        real_part = jnp.dot(tile_wide[0], factor[0]) - jnp.dot(tile_wide[1], factor[1])
        imag_part = jnp.dot(tile_wide[0], factor[1]) + jnp.dot(tile_wide[1], factor[0])
        update = jnp.stack([real_part, imag_part], axis=0)
        column = column.at[block_row].add(update)
        return column, None

    start_column = jnp.zeros((BR_DEV * N_ROW, 2, B, S), jnp.float32)
    indices = jnp.arange(tile_total, dtype=jnp.int32)
    column, _ = lax.scan(add_tile, start_column, (tiles, tile_slot, tile_col, indices))
    inverse_column = -column
    density_rows = (pole_weight[0] * inverse_column[:, 1] + pole_weight[1] * inverse_column[:, 0]).astype(jnp.bfloat16)
    density_rows = density_rows.reshape(-1, S)
    picked = jnp.take(density_rows, box_orbitals, axis=0)
    projected = jnp.einsum("nas,nap->nsp", picked.astype(jnp.float32), box_basis.astype(jnp.float32))
    density = jnp.sum(supernode_basis.astype(jnp.float32) * projected, axis=1)
    return inverse_column, density
```

```python
import functools

import jax
import jax.numpy as jnp
from jax import lax
from jax.experimental import pallas as pl
from jax.experimental.pallas import tpu as pltpu
from jax.sharding import PartitionSpec as P

BR_DEV = 2
MESH = pl.DeviceIdType.MESH


def log2(value):
    assert value & (value - 1) == 0
    return value.bit_length() - 1


def kernel(
    rows, cols, slot_ref, tcol_ref, weight_ref, panel, tiles, orbitals, basis, super_basis,
    inv_ref, density_ref, *scratch,
):
    lanes_y = 2
    depth_z = rows // lanes_y
    chunk_count = 2 * depth_z - 1
    chunks = scratch[:chunk_count]
    (tile_buf, basis_buf, super_buf, orb_buf, acc, half_in, pick_hot, basis_hot, send_rows, recv_rows,
     local_sem, z_send, z_recv, y_send, y_recv, col_sem, orb_send, orb_recv, row_send, row_recv) = scratch[chunk_count:]
    peers = rows * cols
    r = lax.axis_index("row")
    c = lax.axis_index("col")
    me = r * cols + c
    z = r // lanes_y
    y = r % lanes_y
    shard_rows = panel.shape[3]
    width = panel.shape[4]
    tile_count = tiles.shape[0]
    block = tiles.shape[2]
    half = block // cols
    pair = lanes_y * shard_rows
    boxes, orbs = orbitals.shape
    capacity = send_rows.shape[1]

    def spot(index):
        return {"row": index // cols, "col": index % cols}

    loads = [
        pltpu.make_async_copy(panel.at[0], chunks[0].at[y], local_sem.at[0]),
        pltpu.make_async_copy(tiles, tile_buf, local_sem.at[1]),
        pltpu.make_async_copy(basis, basis_buf, local_sem.at[2]),
        pltpu.make_async_copy(super_basis, super_buf, local_sem.at[3]),
        pltpu.make_async_copy(orbitals, orb_buf.at[me], local_sem.at[4]),
    ]
    for load in loads:
        load.start()
    acc[...] = jnp.zeros_like(acc)

    barrier = pltpu.get_barrier_semaphore()
    for k in range(1, peers):
        pl.semaphore_signal(barrier, inc=1, device_id=spot((me + k) % peers), device_id_type=MESH)
    pl.semaphore_wait(barrier, peers - 1)

    def up(d):
        return d

    def down(d):
        return d if d == 0 else depth_z - 1 + d

    def z_copy(kind, d, towards):
        ident = up if kind == "up" else down
        side = 0 if kind == "up" else 1
        src = panel.at[0] if d == 0 else chunks[ident(d)].at[y]
        return pltpu.make_async_remote_copy(
            src_ref=src, dst_ref=chunks[ident(d + 1)].at[y],
            send_sem=z_send.at[side, d], recv_sem=z_recv.at[side, d + 1],
            device_id={"row": towards}, device_id_type=MESH,
        )

    def z_arrival(kind, d):
        ident = up if kind == "up" else down
        side = 0 if kind == "up" else 1
        dst = chunks[ident(d)].at[y]
        return pltpu.make_async_remote_copy(
            src_ref=dst, dst_ref=dst, send_sem=z_send.at[side, d - 1], recv_sem=z_recv.at[side, d],
            device_id={"row": r}, device_id_type=MESH,
        )

    other = r + 1 - 2 * y

    def y_copy(ident):
        src = panel.at[0] if ident == 0 else chunks[ident].at[y]
        return pltpu.make_async_remote_copy(
            src_ref=src, dst_ref=chunks[ident].at[y],
            send_sem=y_send.at[ident], recv_sem=y_recv.at[ident],
            device_id={"row": other}, device_id_type=MESH,
        )

    def y_arrival(ident):
        dst = chunks[ident].at[1 - y]
        return pltpu.make_async_remote_copy(
            src_ref=dst, dst_ref=dst, send_sem=y_send.at[ident], recv_sem=y_recv.at[ident],
            device_id={"row": other}, device_id_type=MESH,
        )

    def has(kind, d):
        return z - d >= 0 if kind == "up" else z + d < depth_z

    def can_send(kind):
        return z + 1 < depth_z if kind == "up" else z >= 1

    def next_row(kind):
        return r + lanes_y if kind == "up" else r - lanes_y

    def forward(kind, d):
        @pl.when(jnp.logical_and(has(kind, d), can_send(kind)))
        def _():
            z_copy(kind, d, next_row(kind)).start()

    def compute(ident, at_z):
        offset = pl.multiple_of(at_z * pair, pair)
        chunk = chunks[ident]

        def one(t, carry):
            j = tcol_ref[t]
            slot = slot_ref[t]
            left = jnp.concatenate(
                [tile_buf[t, 0, :, pl.ds(offset, pair)], tile_buf[t, 1, :, pl.ds(offset, pair)]], axis=1)
            parts = [chunk[k, j] for k in range(lanes_y)]
            real = jnp.concatenate([p[0] for p in parts], axis=0)
            imag = jnp.concatenate([p[1] for p in parts], axis=0)
            right = jnp.concatenate(
                [jnp.concatenate([real, imag], axis=1), jnp.concatenate([-imag, real], axis=1)], axis=0)
            value = jnp.dot(left, right, preferred_element_type=jnp.float32)
            for s in range(BR_DEV):
                acc[s] += jnp.where(slot == s, value, 0.0)
            return carry

        lax.fori_loop(0, tile_count, one, 0)

    forward("up", 0)
    forward("down", 0)
    y_copy(0).start()
    orb_copies = []
    for k in range(1, peers):
        target = (me + k) % peers
        orb_copies.append(pltpu.make_async_remote_copy(
            src_ref=orbitals, dst_ref=orb_buf.at[me], send_sem=orb_send.at[k], recv_sem=orb_recv.at[k],
            device_id=spot(target), device_id_type=MESH,
        ))
        orb_copies[-1].start()

    loads[0].wait()

    def prepare():
        for k in range(1, peers):
            origin = (me + peers - k) % peers
            dst = orb_buf.at[origin]
            pltpu.make_async_remote_copy(
                src_ref=orbitals, dst_ref=dst, send_sem=orb_send.at[k], recv_sem=orb_recv.at[k],
                device_id=spot(origin), device_id_type=MESH,
            ).wait()
        loads[4].wait()
        loads[2].wait()
        block_bits, half_bits = log2(block), log2(half)

        def split(g):
            row_block = g >> block_bits
            within = g & (block - 1)
            source = (row_block >> log2(BR_DEV)) * cols + (within >> half_bits)
            local = (row_block & (BR_DEV - 1)) * half + (within & (half - 1))
            return source, local

        before = lax.broadcasted_iota(jnp.int32, (orbs, orbs), 0)
        after = lax.broadcasted_iota(jnp.int32, (orbs, orbs), 1)
        upper = jnp.where(before <= after, 1.0, 0.0).astype(jnp.bfloat16)

        def ranks(masks):
            seen = jnp.zeros((masks[0].shape[0], 1), jnp.float32)
            result = []
            for mask in masks:
                counted = jnp.dot(mask.astype(jnp.bfloat16), upper, preferred_element_type=jnp.float32)
                result.append(counted - 1.0 + seen)
                seen = seen + jnp.sum(mask, axis=1, keepdims=True)
            return result

        asked = []
        for n in range(boxes):
            g = jnp.concatenate([orb_buf[q, n:n + 1, :] for q in range(peers)], axis=0)
            source, local = split(g)
            asked.append((jnp.where(source == me, 1.0, 0.0), local.astype(jnp.float32)))
        order = ranks([a[0] for a in asked])
        order = [jnp.where(a[0] > 0.5, o, -1.0) for a, o in zip(asked, order)]
        place = lax.broadcasted_iota(jnp.int32, (capacity, orbs), 0).astype(jnp.float32)
        row_id = lax.broadcasted_iota(jnp.int32, (capacity, BR_DEV * half), 1).astype(jnp.float32)
        for q in range(peers):
            found = jnp.zeros((capacity, 1), jnp.float32)
            for n in range(boxes):
                hit = place == order[n][q:q + 1]
                found = found + jnp.sum(jnp.where(hit, asked[n][1][q:q + 1] + 1.0, 0.0), axis=1, keepdims=True)
            pick_hot[q * capacity:(q + 1) * capacity, :] = jnp.where(
                row_id == found - 1.0, 1.0, 0.0).astype(jnp.bfloat16)

        masks = []
        peer_id = lax.broadcasted_iota(jnp.int32, (peers, orbs), 0)
        for n in range(boxes):
            source, _ = split(orb_buf[me, n:n + 1, :])
            masks.append(jnp.where(peer_id == source, 1.0, 0.0))
        order = ranks(masks)
        arrive = lax.broadcasted_iota(jnp.int32, (peers * capacity, orbs), 0).astype(jnp.float32)
        for n in range(boxes):
            position = jnp.sum(
                masks[n] * (order[n] + (peer_id * capacity).astype(jnp.float32)), axis=0, keepdims=True)
            hot = jnp.where(arrive == position, 1.0, 0.0).astype(jnp.bfloat16)
            basis_hot[n] = jnp.dot(hot, basis_buf[n], preferred_element_type=jnp.float32).astype(jnp.bfloat16)

    for d in range(1, depth_z + 1):
        if d < depth_z:
            for kind, ident in (("up", up(d)), ("down", down(d))):
                @pl.when(has(kind, d))
                def _(kind=kind, ident=ident):
                    z_arrival(kind, d).wait_recv()
                    y_copy(ident).start()
                if d < depth_z - 1:
                    forward(kind, d)
        if d == 1:
            y_arrival(0).wait_recv()
            loads[1].wait()
            compute(0, z)
            prepare()
        else:
            for kind, ident, at_z in (("up", up(d - 1), z - d + 1), ("down", down(d - 1), z + d - 1)):
                @pl.when(has(kind, d - 1))
                def _(ident=ident, at_z=at_z):
                    y_arrival(ident).wait_recv()
                    compute(ident, at_z)

    mine = pl.ds(pl.multiple_of(c * half, half), half)
    theirs = pl.ds(pl.multiple_of((1 - c) * half, half), half)
    swap = pltpu.make_async_remote_copy(
        src_ref=acc.at[:, theirs, :], dst_ref=half_in, send_sem=col_sem.at[0], recv_sem=col_sem.at[1],
        device_id={"col": 1 - c}, device_id_type=MESH,
    )
    swap.start()
    swap.wait_recv()
    density_rows = []
    for s in range(BR_DEV):
        column = -(acc[s, mine, :] + half_in[s])
        real, imag = column[:, :width], column[:, width:]
        inv_ref[s, 0] = real
        inv_ref[s, 1] = imag
        density_rows.append((weight_ref[0] * imag + weight_ref[1] * real).astype(jnp.bfloat16))
    density_rows = jnp.concatenate(density_rows, axis=0)
    picked = jnp.dot(pick_hot[...], density_rows, preferred_element_type=jnp.float32).astype(jnp.bfloat16)
    send_rows[...] = picked.reshape(send_rows.shape)
    row_copies = []
    for k in range(1, peers):
        target = (me + k) % peers
        row_copies.append(pltpu.make_async_remote_copy(
            src_ref=send_rows.at[target], dst_ref=recv_rows.at[me],
            send_sem=row_send.at[k], recv_sem=row_recv.at[k],
            device_id=spot(target), device_id_type=MESH,
        ))
        row_copies[-1].start()
    recv_rows[me] = send_rows[me]
    loads[3].wait()
    for k in range(1, peers):
        origin = (me + peers - k) % peers
        dst = recv_rows.at[origin]
        pltpu.make_async_remote_copy(
            src_ref=dst, dst_ref=dst, send_sem=row_send.at[k], recv_sem=row_recv.at[k],
            device_id=spot(origin), device_id_type=MESH,
        ).wait_recv()
    arrived = recv_rows[...].reshape(peers * capacity, width)
    for n in range(boxes):
        projected = lax.dot_general(
            arrived, basis_hot[n], (((0,), (0,)), ((), ())), preferred_element_type=jnp.float32)
        density_ref[n:n + 1, :] = jnp.sum(
            super_buf[n].astype(jnp.float32) * projected, axis=0, keepdims=True)

    for kind in ("up", "down"):
        for d in range(depth_z - 1):
            @pl.when(jnp.logical_and(has(kind, d), can_send(kind)))
            def _(kind=kind, d=d):
                z_copy(kind, d, next_row(kind)).wait_send()
    y_copy(0).wait_send()
    for d in range(1, depth_z):
        for kind, ident in (("up", up(d)), ("down", down(d))):
            @pl.when(has(kind, d))
            def _(ident=ident):
                y_copy(ident).wait_send()
    swap.wait_send()
    for copy in row_copies:
        copy.wait_send()


def fused(rows, cols, panel, tiles, tile_slot, tile_col, pole_weight, box_orbitals, box_basis, supernode_basis):
    blocks, parts, shard_rows, width = panel.shape[1:]
    tile_count, _, block, _ = tiles.shape
    boxes, orbs = box_orbitals.shape
    points = box_basis.shape[2]
    half = block // cols
    peers = rows * cols
    capacity = 2 * boxes * orbs // peers
    depth_z = rows // 2
    dma = pltpu.SemaphoreType.DMA
    bf16, f32 = jnp.bfloat16, jnp.float32
    smem = pl.BlockSpec(memory_space=pltpu.SMEM)
    hbm = pl.BlockSpec(memory_space=pl.ANY)
    vmem = pl.BlockSpec(memory_space=pltpu.VMEM)
    return pl.pallas_call(
        functools.partial(kernel, rows, cols),
        name="pole_step",
        out_shape=(
            jax.ShapeDtypeStruct((BR_DEV, 2, half, width), f32),
            jax.ShapeDtypeStruct((boxes, points), f32),
        ),
        in_specs=[smem] * 3 + [hbm] * 5,
        out_specs=(vmem, vmem),
        scratch_shapes=[pltpu.VMEM((2, blocks, parts, shard_rows, width), bf16)] * (2 * depth_z - 1) + [
            pltpu.VMEM(tiles.shape, bf16),
            pltpu.VMEM(box_basis.shape, bf16),
            pltpu.VMEM(supernode_basis.shape, bf16),
            pltpu.VMEM((peers, boxes, orbs), jnp.int32),
            pltpu.VMEM((BR_DEV, block, 2 * width), f32),
            pltpu.VMEM((BR_DEV, half, 2 * width), f32),
            pltpu.VMEM((peers * capacity, BR_DEV * half), bf16),
            pltpu.VMEM((boxes, peers * capacity, points), bf16),
            pltpu.VMEM((peers, capacity, width), bf16),
            pltpu.VMEM((peers, capacity, width), bf16),
            dma((5,)),
            dma((2, depth_z)),
            dma((2, depth_z)),
            dma((2 * depth_z - 1,)),
            dma((2 * depth_z - 1,)),
            dma((2,)),
            dma((peers,)),
            dma((peers,)),
            dma((peers,)),
            dma((peers,)),
        ],
        compiler_params=pltpu.CompilerParams(
            collective_id=0, has_side_effects=True, vmem_limit_bytes=56 * 1024 * 1024),
    )(tile_slot, tile_col, pole_weight, panel, tiles, box_orbitals, box_basis, supernode_basis)


def plain(panel, tiles, tile_slot, tile_col, pole_weight, box_orbitals, box_basis, supernode_basis):
    gathered = lax.all_gather(panel, "row", axis=3, tiled=True)
    blocks = gathered[0]
    selector = (tile_col[:, None] == jnp.arange(blocks.shape[0], dtype=jnp.int32)[None, :]).astype(
        jnp.bfloat16
    )
    chosen = jnp.einsum(
        "tj,jcbs->tcbs", selector, blocks, preferred_element_type=jnp.float32
    ).astype(jnp.bfloat16)
    real_part = jnp.einsum(
        "tab,tbs->tas", tiles[:, 0], chosen[:, 0], preferred_element_type=jnp.float32
    )
    real_part = real_part - jnp.einsum(
        "tab,tbs->tas", tiles[:, 1], chosen[:, 1], preferred_element_type=jnp.float32
    )
    imag_part = jnp.einsum(
        "tab,tbs->tas", tiles[:, 0], chosen[:, 1], preferred_element_type=jnp.float32
    )
    imag_part = imag_part + jnp.einsum(
        "tab,tbs->tas", tiles[:, 1], chosen[:, 0], preferred_element_type=jnp.float32
    )
    products = jnp.stack([real_part, imag_part], axis=1)
    partial_value = jnp.stack(
        [
            jnp.sum(jnp.where((tile_slot == slot_row)[:, None, None, None], products, 0.0), axis=0)
            for slot_row in range(BR_DEV)
        ]
    )
    summed = lax.psum_scatter(partial_value, "col", scatter_dimension=2, tiled=True)
    inverse_column = -summed
    density_local = (
        pole_weight[0] * inverse_column[:, 1] + pole_weight[1] * inverse_column[:, 0]
    ).astype(jnp.bfloat16)
    columns = density_local.shape[2]
    density_local = density_local.reshape(-1, columns)
    block_width = tiles.shape[2]
    col_count = lax.axis_size("col")
    half_rows = block_width // col_count
    wanted = box_orbitals.reshape(-1)
    wanted_total = wanted.shape[0]
    block_index = wanted // block_width
    within = wanted % block_width
    source = block_index // BR_DEV * col_count + within // half_rows
    local_row = block_index % BR_DEV * half_rows + within % half_rows
    start_rows = jnp.zeros((wanted_total, columns), jnp.bfloat16)
    shards = lax.all_gather(density_local[None], ("row", "col"), axis=0, tiled=True)
    count = shards.shape[0]
    inside = (source >= 0) & (source < count)
    clipped = jnp.clip(source, 0, count - 1)
    fetched = shards[clipped, local_row]
    picked = jnp.where(inside[:, None], fetched, start_rows)
    picked = picked.reshape(box_basis.shape[0], box_basis.shape[1], columns)
    projected = jnp.einsum("nas,nap->nsp", picked, box_basis, preferred_element_type=jnp.float32)
    density = jnp.sum(supernode_basis.astype(jnp.float32) * projected, axis=1)
    return (inverse_column, density)


def solution(mesh):
    rows, cols = mesh.shape["row"], mesh.shape["col"]

    def local(panel, *rest):
        if cols == 2 and rows % 2 == 0 and 2 * panel.shape[3] % panel.shape[4] == 0:
            return fused(rows, cols, panel, *rest)
        return plain(panel, *rest)

    return jax.shard_map(
        local,
        mesh=mesh,
        in_specs=(
            P(("pole", "col"), None, None, "row", None),
            P(("pole", "row", "col"), None, None, None),
            P(("pole", "row", "col")),
            P(("pole", "row", "col")),
            P("pole"),
            P(("pole", "row", "col"), None),
            P(("pole", "row", "col"), None, None),
            P(("pole", "row", "col"), None, None),
        ),
        out_specs=(P(("pole", "row"), None, "col", None), P(("pole", "row", "col"), None)),
        check_vma=False,
    )
```

```python
import functools

import jax
import jax.numpy as jnp
from jax import lax
from jax.experimental import pallas as pl
from jax.experimental.pallas import tpu as pltpu
from jax.sharding import PartitionSpec as P

BR_DEV = 2
MESH = pl.DeviceIdType.MESH


def log2(value):
    assert value & (value - 1) == 0
    return value.bit_length() - 1


def kernel(
    rows, cols, slot_ref, tcol_ref, weight_ref, panel, tiles, orbitals, basis, super_basis,
    inv_ref, density_ref, *scratch,
):
    lanes_y = 2
    depth_z = rows // lanes_y
    chunk_count = 2 * depth_z - 1
    chunks = scratch[:chunk_count]
    (tile_buf, basis_buf, super_buf, orb_buf, acc, half_in, pick_hot, basis_hot, send_rows, recv_rows,
     local_sem, z_send, z_recv, y_send, y_recv, x_send, x_recv, col_sem, orb_send, orb_recv, row_send, row_recv) = scratch[chunk_count:]
    peers = rows * cols
    r = lax.axis_index("row")
    c = lax.axis_index("col")
    me = r * cols + c
    z = r // lanes_y
    y = r % lanes_y
    shard_rows = panel.shape[3]
    width = panel.shape[4]
    tile_count = tiles.shape[0]
    block = tiles.shape[2]
    half = block // cols
    pair = lanes_y * shard_rows
    boxes, orbs = orbitals.shape
    capacity = send_rows.shape[1]
    pieces = z_send.shape[2]
    late = pieces // 2
    step = panel.shape[1] // pieces

    def spot(index):
        return {"row": index // cols, "col": index % cols}

    loads = [
        pltpu.make_async_copy(panel.at[0], chunks[0].at[y], local_sem.at[0]),
        pltpu.make_async_copy(tiles, tile_buf, local_sem.at[1]),
        pltpu.make_async_copy(basis, basis_buf, local_sem.at[2]),
        pltpu.make_async_copy(super_basis, super_buf, local_sem.at[3]),
        pltpu.make_async_copy(orbitals, orb_buf.at[me], local_sem.at[4]),
    ]
    for load in loads:
        load.start()
    acc[...] = jnp.zeros_like(acc)

    barrier = pltpu.get_barrier_semaphore()
    for k in range(1, peers):
        pl.semaphore_signal(barrier, inc=1, device_id=spot((me + k) % peers), device_id_type=MESH)
    pl.semaphore_wait(barrier, peers - 1)

    def up(d):
        return d

    def down(d):
        return d if d == 0 else depth_z - 1 + d

    idents = {"up": up, "down": down}
    sides = {"up": 0, "down": 1}
    other = r + 1 - 2 * y
    partner = r + lanes_y - 2 * lanes_y * (z % 2)

    def has(kind, d):
        return z - d >= 0 if kind == "up" else z + d < depth_z

    def can_send(kind):
        return z + 1 < depth_z if kind == "up" else z >= 1

    def from_partner(kind):
        return z % 2 == 1 if kind == "up" else z % 2 == 0

    def piece(ref, h):
        return ref.at[pl.ds(h * step, step)]

    def z_copy(kind, d, h):
        side = sides[kind]
        src = panel.at[0] if d == 0 else chunks[idents[kind](d)].at[y]
        return pltpu.make_async_remote_copy(
            src_ref=piece(src, h), dst_ref=piece(chunks[idents[kind](d + 1)].at[y], h),
            send_sem=z_send.at[side, d, h], recv_sem=z_recv.at[side, d + 1, h],
            device_id={"row": r + lanes_y if kind == "up" else r - lanes_y}, device_id_type=MESH,
        )

    def z_arrival(kind, d, h):
        side = sides[kind]
        dst = piece(chunks[idents[kind](d)].at[y], h)
        return pltpu.make_async_remote_copy(
            src_ref=dst, dst_ref=dst, send_sem=z_send.at[side, d - 1, h], recv_sem=z_recv.at[side, d, h],
            device_id={"row": other}, device_id_type=MESH,
        )

    def y_copy(ident, h):
        src = panel.at[0] if ident == 0 else chunks[ident].at[y]
        return pltpu.make_async_remote_copy(
            src_ref=piece(src, h), dst_ref=piece(chunks[ident].at[y], h),
            send_sem=y_send.at[ident, h], recv_sem=y_recv.at[ident, h],
            device_id={"row": other}, device_id_type=MESH,
        )

    def y_arrival(ident, h):
        dst = piece(chunks[ident].at[1 - y], h)
        return pltpu.make_async_remote_copy(
            src_ref=dst, dst_ref=dst, send_sem=y_send.at[ident, h], recv_sem=y_recv.at[ident, h],
            device_id={"row": other}, device_id_type=MESH,
        )

    def extra_copy(kind, h):
        return pltpu.make_async_remote_copy(
            src_ref=piece(chunks[0].at[1 - y], h), dst_ref=piece(chunks[idents[kind](1)].at[1 - y], h),
            send_sem=x_send.at[h], recv_sem=x_recv.at[h],
            device_id={"row": partner}, device_id_type=MESH,
        )

    def extra_arrival(kind, h):
        dst = piece(chunks[idents[kind](1)].at[1 - y], h)
        return pltpu.make_async_remote_copy(
            src_ref=dst, dst_ref=dst, send_sem=x_send.at[h], recv_sem=x_recv.at[h],
            device_id={"row": partner}, device_id_type=MESH,
        )

    def each(low, high, body):
        def run(h, carry):
            body(h)
            return carry
        lax.fori_loop(low, high, run, 0)

    def y_forward(kind, d, h, act):
        ident = idents[kind](d)
        if d == 1:
            @pl.when(jnp.logical_or(jnp.logical_not(from_partner(kind)), h < late))
            def _():
                act(y_copy(ident, h))
        else:
            act(y_copy(ident, h))

    def chunk_ready(kind, d):
        ident = idents[kind](d)
        each(0, late if d == 1 else pieces, lambda h: y_arrival(ident, h).wait_recv())
        if d == 1:
            @pl.when(from_partner(kind))
            def _():
                each(late, pieces, lambda h: extra_arrival(kind, h).wait_recv())

            @pl.when(jnp.logical_not(from_partner(kind)))
            def _():
                each(late, pieces, lambda h: y_arrival(ident, h).wait_recv())

    def compute(ident, at_z, first, last, group=1):
        offset = pl.multiple_of(at_z * pair, pair)
        chunk = chunks[ident]

        def product(t):
            j = tcol_ref[t]
            left = jnp.concatenate(
                [tile_buf[t, 0, :, pl.ds(offset, pair)], tile_buf[t, 1, :, pl.ds(offset, pair)]], axis=1)
            parts = [chunk[k, j] for k in range(lanes_y)]
            real = jnp.concatenate([p[0] for p in parts], axis=0)
            imag = jnp.concatenate([p[1] for p in parts], axis=0)
            right = jnp.concatenate(
                [jnp.concatenate([real, imag], axis=1), jnp.concatenate([-imag, real], axis=1)], axis=0)
            return jnp.dot(left, right, preferred_element_type=jnp.float32)

        def several(start, count):
            values = [product(start + k) for k in range(count)]
            for s in range(BR_DEV):
                total = jnp.where(slot_ref[start] == s, values[0], 0.0)
                for k in range(1, count):
                    total = total + jnp.where(slot_ref[start + k] == s, values[k], 0.0)
                acc[s] += total

        if group == 1:
            each(first, last, lambda t: several(t, 1))
        else:
            for start in range(first, last, group):
                several(start, min(group, last - start))

    def at(kind, d):
        return z - d if kind == "up" else z + d

    orb_copies = []
    for k in range(1, peers):
        target = (me + k) % peers
        orb_copies.append(pltpu.make_async_remote_copy(
            src_ref=orbitals, dst_ref=orb_buf.at[me], send_sem=orb_send.at[k], recv_sem=orb_recv.at[k],
            device_id=spot(target), device_id_type=MESH,
        ))
        orb_copies[-1].start()

    def own_z(h):
        for kind in idents:
            @pl.when(can_send(kind))
            def _(kind=kind):
                z_copy(kind, 0, h).start()

    def own_piece(h):
        own_z(h)
        y_copy(0, (h + late) % pieces).start()

    each(0, pieces, own_piece)
    loads[0].wait()

    def prepare():
        for k in range(1, peers):
            origin = (me + peers - k) % peers
            dst = orb_buf.at[origin]
            pltpu.make_async_remote_copy(
                src_ref=orbitals, dst_ref=dst, send_sem=orb_send.at[k], recv_sem=orb_recv.at[k],
                device_id=spot(origin), device_id_type=MESH,
            ).wait()
        loads[4].wait()
        loads[2].wait()
        block_bits, half_bits = log2(block), log2(half)

        def split(g):
            row_block = g >> block_bits
            within = g & (block - 1)
            source = (row_block >> log2(BR_DEV)) * cols + (within >> half_bits)
            local = (row_block & (BR_DEV - 1)) * half + (within & (half - 1))
            return source, local

        before = lax.broadcasted_iota(jnp.int32, (orbs, orbs), 0)
        after = lax.broadcasted_iota(jnp.int32, (orbs, orbs), 1)
        upper = jnp.where(before <= after, 1.0, 0.0).astype(jnp.bfloat16)

        def ranks(masks):
            seen = jnp.zeros((masks[0].shape[0], 1), jnp.float32)
            result = []
            for mask in masks:
                counted = jnp.dot(mask.astype(jnp.bfloat16), upper, preferred_element_type=jnp.float32)
                result.append(counted - 1.0 + seen)
                seen = seen + jnp.sum(mask, axis=1, keepdims=True)
            return result

        asked = []
        for n in range(boxes):
            g = jnp.concatenate([orb_buf[q, n:n + 1, :] for q in range(peers)], axis=0)
            source, local = split(g)
            asked.append((jnp.where(source == me, 1.0, 0.0), local.astype(jnp.float32)))
        order = ranks([a[0] for a in asked])
        order = [jnp.where(a[0] > 0.5, o, -1.0) for a, o in zip(asked, order)]
        place = lax.broadcasted_iota(jnp.int32, (capacity, orbs), 0).astype(jnp.float32)
        row_id = lax.broadcasted_iota(jnp.int32, (capacity, BR_DEV * half), 1).astype(jnp.float32)
        for q in range(peers):
            found = jnp.zeros((capacity, 1), jnp.float32)
            for n in range(boxes):
                hit = place == order[n][q:q + 1]
                found = found + jnp.sum(jnp.where(hit, asked[n][1][q:q + 1] + 1.0, 0.0), axis=1, keepdims=True)
            pick_hot[q * capacity:(q + 1) * capacity, :] = jnp.where(
                row_id == found - 1.0, 1.0, 0.0).astype(jnp.bfloat16)

        masks = []
        peer_id = lax.broadcasted_iota(jnp.int32, (peers, orbs), 0)
        for n in range(boxes):
            source, _ = split(orb_buf[me, n:n + 1, :])
            masks.append(jnp.where(peer_id == source, 1.0, 0.0))
        order = ranks(masks)
        arrive = lax.broadcasted_iota(jnp.int32, (peers * capacity, orbs), 0).astype(jnp.float32)
        for n in range(boxes):
            position = jnp.sum(
                masks[n] * (order[n] + (peer_id * capacity).astype(jnp.float32)), axis=0, keepdims=True)
            hot = jnp.where(arrive == position, 1.0, 0.0).astype(jnp.bfloat16)
            basis_hot[n] = jnp.dot(hot, basis_buf[n], preferred_element_type=jnp.float32).astype(jnp.bfloat16)

    def send_extra(h):
        y_arrival(0, h).wait_recv()
        for kind in idents:
            @pl.when(jnp.logical_not(from_partner(kind)))
            def _(kind=kind):
                extra_copy(kind, h).start()

    each(late, pieces, send_extra)
    prepare()
    for d in range(1, depth_z):
        if d == 2:
            each(0, late, lambda h: y_arrival(0, h).wait_recv())
            loads[1].wait()
        if d >= 3:
            for kind in idents:
                @pl.when(has(kind, d - 2))
                def _(kind=kind):
                    chunk_ready(kind, d - 2)

        final = d >= 3 and d == depth_z - 1

        def arrive_piece(h, d=d, final=final, behind=2):
            for kind in idents:
                @pl.when(has(kind, d))
                def _(kind=kind):
                    z_arrival(kind, d, h).wait_recv()
                    if d < depth_z - 1:
                        @pl.when(can_send(kind))
                        def _():
                            z_copy(kind, d, h).start()
                    y_forward(kind, d, h, lambda copy: copy.start())
            first, last = h * tile_count // pieces, (h + 1) * tile_count // pieces
            if d == 2:
                compute(0, z, first, last)
            if final:
                done = h - (0 if behind == 2 else late)
                first, last = done * tile_count // late, (done + 1) * tile_count // late
            if d >= 3:
                for kind in idents:
                    @pl.when(has(kind, d if behind == 1 else d - 2))
                    def _(kind=kind):
                        compute(idents[kind](d - behind), at(kind, d - behind), first, last)

        if final:
            each(0, late, arrive_piece)
            for kind in idents:
                @pl.when(has(kind, d))
                def _(kind=kind, d=d):
                    chunk_ready(kind, d - 1)
            each(late, pieces, functools.partial(arrive_piece, behind=1))
        else:
            each(0, pieces, arrive_piece)
    if depth_z == 2:
        each(0, late, lambda h: y_arrival(0, h).wait_recv())
        loads[1].wait()
        compute(0, z, 0, tile_count)
    for d in range(max(depth_z - 2, 1), depth_z):
        for kind in idents:
            waiting = has(kind, d)
            if depth_z >= 4 and d == depth_z - 2:
                waiting = jnp.logical_and(waiting, jnp.logical_not(has(kind, d + 1)))

            @pl.when(waiting)
            def _(kind=kind, d=d):
                chunk_ready(kind, d)
                compute(idents[kind](d), at(kind, d), 0, tile_count, group=4)

    mine = pl.ds(pl.multiple_of(c * half, half), half)
    theirs = pl.ds(pl.multiple_of((1 - c) * half, half), half)
    swap = pltpu.make_async_remote_copy(
        src_ref=acc.at[:, theirs, :], dst_ref=half_in, send_sem=col_sem.at[0], recv_sem=col_sem.at[1],
        device_id={"col": 1 - c}, device_id_type=MESH,
    )
    swap.start()
    swap.wait_recv()
    density_rows = []
    for s in range(BR_DEV):
        column = -(acc[s, mine, :] + half_in[s])
        real, imag = column[:, :width], column[:, width:]
        density_rows.append((weight_ref[0] * imag + weight_ref[1] * real).astype(jnp.bfloat16))
    density_rows = jnp.concatenate(density_rows, axis=0)
    picked = jnp.dot(pick_hot[...], density_rows, preferred_element_type=jnp.float32).astype(jnp.bfloat16)
    send_rows[...] = picked.reshape(send_rows.shape)
    row_copies = []
    for k in range(1, peers):
        target = (me + k) % peers
        row_copies.append(pltpu.make_async_remote_copy(
            src_ref=send_rows.at[target], dst_ref=recv_rows.at[me],
            send_sem=row_send.at[k], recv_sem=row_recv.at[k],
            device_id=spot(target), device_id_type=MESH,
        ))
        row_copies[-1].start()
    recv_rows[me] = send_rows[me]
    for s in range(BR_DEV):
        column = -(acc[s, mine, :] + half_in[s])
        inv_ref[s, 0] = column[:, :width]
        inv_ref[s, 1] = column[:, width:]
    loads[3].wait()
    for k in range(1, peers):
        origin = (me + peers - k) % peers
        dst = recv_rows.at[origin]
        pltpu.make_async_remote_copy(
            src_ref=dst, dst_ref=dst, send_sem=row_send.at[k], recv_sem=row_recv.at[k],
            device_id=spot(origin), device_id_type=MESH,
        ).wait_recv()
    arrived = recv_rows[...].reshape(peers * capacity, width)
    for n in range(boxes):
        projected = lax.dot_general(
            arrived, basis_hot[n], (((0,), (0,)), ((), ())), preferred_element_type=jnp.float32)
        density_ref[n:n + 1, :] = jnp.sum(
            super_buf[n].astype(jnp.float32) * projected, axis=0, keepdims=True)

    def sent(h):
        y_copy(0, h).wait_send()
        for kind in idents:
            for d in range(depth_z - 1):
                @pl.when(jnp.logical_and(has(kind, d), can_send(kind)))
                def _(kind=kind, d=d):
                    z_copy(kind, d, h).wait_send()
            for d in range(1, depth_z):
                @pl.when(has(kind, d))
                def _(kind=kind, d=d):
                    y_forward(kind, d, h, lambda copy: copy.wait_send())

    each(0, pieces, sent)

    def extra_sent(h):
        for kind in idents:
            @pl.when(jnp.logical_not(from_partner(kind)))
            def _(kind=kind):
                extra_copy(kind, h).wait_send()

    each(late, pieces, extra_sent)
    swap.wait_send()
    for copy in row_copies:
        copy.wait_send()


def fused(rows, cols, panel, tiles, tile_slot, tile_col, pole_weight, box_orbitals, box_basis, supernode_basis):
    blocks, parts, shard_rows, width = panel.shape[1:]
    tile_count, _, block, _ = tiles.shape
    boxes, orbs = box_orbitals.shape
    points = box_basis.shape[2]
    half = block // cols
    peers = rows * cols
    capacity = 2 * boxes * orbs // peers
    depth_z = rows // 2
    pieces = blocks // 2
    dma = pltpu.SemaphoreType.DMA
    bf16, f32 = jnp.bfloat16, jnp.float32
    smem = pl.BlockSpec(memory_space=pltpu.SMEM)
    hbm = pl.BlockSpec(memory_space=pl.ANY)
    vmem = pl.BlockSpec(memory_space=pltpu.VMEM)
    return pl.pallas_call(
        functools.partial(kernel, rows, cols),
        name="pole_step",
        out_shape=(
            jax.ShapeDtypeStruct((BR_DEV, 2, half, width), f32),
            jax.ShapeDtypeStruct((boxes, points), f32),
        ),
        in_specs=[smem] * 3 + [hbm] * 5,
        out_specs=(vmem, vmem),
        scratch_shapes=[pltpu.VMEM((2, blocks, parts, shard_rows, width), bf16)] * (2 * depth_z - 1) + [
            pltpu.VMEM(tiles.shape, bf16),
            pltpu.VMEM(box_basis.shape, bf16),
            pltpu.VMEM(supernode_basis.shape, bf16),
            pltpu.VMEM((peers, boxes, orbs), jnp.int32),
            pltpu.VMEM((BR_DEV, block, 2 * width), f32),
            pltpu.VMEM((BR_DEV, half, 2 * width), f32),
            pltpu.VMEM((peers * capacity, BR_DEV * half), bf16),
            pltpu.VMEM((boxes, peers * capacity, points), bf16),
            pltpu.VMEM((peers, capacity, width), bf16),
            pltpu.VMEM((peers, capacity, width), bf16),
            dma((5,)),
            dma((2, depth_z, pieces)),
            dma((2, depth_z, pieces)),
            dma((2 * depth_z - 1, pieces)),
            dma((2 * depth_z - 1, pieces)),
            dma((pieces,)),
            dma((pieces,)),
            dma((2,)),
            dma((peers,)),
            dma((peers,)),
            dma((peers,)),
            dma((peers,)),
        ],
        compiler_params=pltpu.CompilerParams(
            collective_id=0, has_side_effects=True, vmem_limit_bytes=56 * 1024 * 1024),
    )(tile_slot, tile_col, pole_weight, panel, tiles, box_orbitals, box_basis, supernode_basis)


def plain(panel, tiles, tile_slot, tile_col, pole_weight, box_orbitals, box_basis, supernode_basis):
    gathered = lax.all_gather(panel, "row", axis=3, tiled=True)
    blocks = gathered[0]
    selector = (tile_col[:, None] == jnp.arange(blocks.shape[0], dtype=jnp.int32)[None, :]).astype(
        jnp.bfloat16
    )
    chosen = jnp.einsum(
        "tj,jcbs->tcbs", selector, blocks, preferred_element_type=jnp.float32
    ).astype(jnp.bfloat16)
    real_part = jnp.einsum(
        "tab,tbs->tas", tiles[:, 0], chosen[:, 0], preferred_element_type=jnp.float32
    )
    real_part = real_part - jnp.einsum(
        "tab,tbs->tas", tiles[:, 1], chosen[:, 1], preferred_element_type=jnp.float32
    )
    imag_part = jnp.einsum(
        "tab,tbs->tas", tiles[:, 0], chosen[:, 1], preferred_element_type=jnp.float32
    )
    imag_part = imag_part + jnp.einsum(
        "tab,tbs->tas", tiles[:, 1], chosen[:, 0], preferred_element_type=jnp.float32
    )
    products = jnp.stack([real_part, imag_part], axis=1)
    partial_value = jnp.stack(
        [
            jnp.sum(jnp.where((tile_slot == slot_row)[:, None, None, None], products, 0.0), axis=0)
            for slot_row in range(BR_DEV)
        ]
    )
    summed = lax.psum_scatter(partial_value, "col", scatter_dimension=2, tiled=True)
    inverse_column = -summed
    density_local = (
        pole_weight[0] * inverse_column[:, 1] + pole_weight[1] * inverse_column[:, 0]
    ).astype(jnp.bfloat16)
    columns = density_local.shape[2]
    density_local = density_local.reshape(-1, columns)
    block_width = tiles.shape[2]
    col_count = lax.axis_size("col")
    half_rows = block_width // col_count
    wanted = box_orbitals.reshape(-1)
    wanted_total = wanted.shape[0]
    block_index = wanted // block_width
    within = wanted % block_width
    source = block_index // BR_DEV * col_count + within // half_rows
    local_row = block_index % BR_DEV * half_rows + within % half_rows
    start_rows = jnp.zeros((wanted_total, columns), jnp.bfloat16)
    shards = lax.all_gather(density_local[None], ("row", "col"), axis=0, tiled=True)
    count = shards.shape[0]
    inside = (source >= 0) & (source < count)
    clipped = jnp.clip(source, 0, count - 1)
    fetched = shards[clipped, local_row]
    picked = jnp.where(inside[:, None], fetched, start_rows)
    picked = picked.reshape(box_basis.shape[0], box_basis.shape[1], columns)
    projected = jnp.einsum("nas,nap->nsp", picked, box_basis, preferred_element_type=jnp.float32)
    density = jnp.sum(supernode_basis.astype(jnp.float32) * projected, axis=1)
    return (inverse_column, density)


def solution(mesh):
    rows, cols = mesh.shape["row"], mesh.shape["col"]

    def local(panel, *rest):
        if cols == 2 and rows % 4 == 0 and panel.shape[1] % 4 == 0 and 2 * panel.shape[3] % panel.shape[4] == 0:
            return fused(rows, cols, panel, *rest)
        return plain(panel, *rest)

    return jax.shard_map(
        local,
        mesh=mesh,
        in_specs=(
            P(("pole", "col"), None, None, "row", None),
            P(("pole", "row", "col"), None, None, None),
            P(("pole", "row", "col")),
            P(("pole", "row", "col")),
            P("pole"),
            P(("pole", "row", "col"), None),
            P(("pole", "row", "col"), None, None),
            P(("pole", "row", "col"), None, None),
        ),
        out_specs=(P(("pole", "row"), None, "col", None), P(("pole", "row", "col"), None)),
        check_vma=False,
    )
```
